768 devices in a mesh: grp: 192 (over y, z, core), dev: 4 (over x).
Axes of the slice: x: 4, y: 8, z: 12, core: 2. Of those that a mesh axis runs over, the one named last changes fastest.
Arguments:
- operators: bfloat16 [1536, 1024, 1024], P(('grp', 'dev')), may hold values from -0.3 to 2.3, as said below
- forces: float32 [1536, 32, 512], P(('grp', 'dev')), may hold values from -48 to 48
- weights: float32 [1536, 512], P(('grp', 'dev')), may hold values from 0.5 to 2
- lengths: int32 [1536], replicated, may hold values from 128 to 512, as said below
- slot_order: int32 [1536, 512], P(('grp', 'dev')), may hold values from 0 to 511, as said below
Outputs:
- solution: float32 [1536, 32, 512], P(('grp', 'dev'))
- residual: float32 [1536, 32, 512], P(('grp', 'dev'))
The draws below stay inside these ranges and needn't reach their ends.
Inputs may be any that keep to these rules, and one draw needn't show every extreme that they name: `lengths`: every interface has at least 128 live multipliers and some interface has exactly 512; the last entry belongs to the end of the chain and is not used. `slot_order`: row k is a permutation of 0 to 511 that maps the first lengths[k] positions onto the first lengths[k] slots and leaves the other positions in place. `operators`: each operator is symmetric, and positive definite on every subset of its rows and columns.
All inputs are finite; a program needn't handle non-finite values.
Results may differ from the reference program's by a relative error of at most 0.01.
Values may be sent and summed in bfloat16 or wider, within the bound.
No kernel may reach another device: no remote copies, remote signals or barrier semaphores. Data moves between devices by JAX's collectives and lax.ppermute only.
A program may use at most 32 MiB of HBM per device.

```python
import math
import jax
import jax.numpy as jnp
from jax import lax

IFACE = 512
LOADS = 32
ITERS = 2
NSUB = 1536


def plan_lengths(key):
    first_key, second_key, third_key, fourth_key = jax.random.split(jax.random.fold_in(key, 17), 4)
    heavy = jax.random.randint(first_key, (NSUB,), 0, 4) == 0
    longer = jax.random.randint(second_key, (NSUB,), IFACE // 2 + 1, IFACE + 1)
    shorter = jax.random.randint(third_key, (NSUB,), IFACE // 4, IFACE // 2 + 1)
    drawn = jnp.where(heavy, longer, shorter).astype(jnp.int32)
    chosen = jax.random.randint(fourth_key, (), 0, max(NSUB - 1, 1))
    return drawn.at[chosen].set(IFACE).astype(jnp.int32)


def draw_lengths(key, part):
    return plan_lengths(key)


def draw_slot_order(key, part):
    drawn = plan_lengths(key)
    many_keys = jax.random.split(jax.random.fold_in(key, 29), NSUB)
    rankings = jax.vmap(lambda sub_key: jax.random.permutation(sub_key, IFACE))(many_keys).astype(jnp.int32)
    positions = jnp.arange(IFACE, dtype=jnp.int32)
    scores = jnp.where(positions[None, :] < drawn[:, None], rankings, IFACE + positions[None, :])
    return jnp.argsort(scores, axis=1, stable=True).astype(jnp.int32)


def draw_operators(key, part):
    extent = 2 * IFACE
    spread = 0.35 / math.sqrt(extent)

    def single(subdomain):
        sub_key = jax.random.fold_in(jax.random.fold_in(key, 41), subdomain)
        first_key, second_key = jax.random.split(sub_key)
        noise = jax.random.normal(first_key, (extent, extent), jnp.float32) * spread
        symmetric = (noise + noise.T) / math.sqrt(2.0)
        diagonal = jax.random.uniform(second_key, (extent,), jnp.float32, 1.0, 2.0)
        return (symmetric + jnp.diag(diagonal)).astype(jnp.bfloat16)
    return lax.map(single, jnp.arange(NSUB))


def draw_forces(key, part):
    first_key = jax.random.fold_in(jax.random.fold_in(key, 53), 0)
    growth = 3.0 ** (jnp.arange(NSUB, dtype=jnp.float32) / max(NSUB - 1, 1))
    noise = jnp.clip(jax.random.normal(first_key, (NSUB, LOADS, IFACE), jnp.float32), -6.0, 6.0)
    return noise * growth[:, None, None]


def steps_of(rng, shape, pieces, smallest, top_value):
    gain = 1.0
    for position, blocks in pieces:
        heights = jax.random.uniform(jax.random.fold_in(jax.random.fold_in(rng, 6), position), (blocks,), jnp.float32, smallest / len(pieces), top_value / len(pieces))
        gain = gain * jnp.repeat(jnp.exp(heights), shape[position] // blocks).reshape((-1,) + (1,) * (len(shape) - 1 - position))
    return gain


def setup_inputs(seed: int = 0) -> dict:
    keys = jax.random.split(jax.random.key(seed), 6)
    return {
        "operators": draw_operators(jax.random.fold_in(keys[5], 71), 0),
        "forces": draw_forces(jax.random.fold_in(keys[5], 71), 0),
        "weights": jnp.clip(jnp.exp(math.log(2.0) - 1.3862944 * jax.random.uniform(keys[2], (NSUB, IFACE), jnp.float32) ** steps_of(keys[2], (NSUB, IFACE), ((0, 768),), -0.2, 0.2)), 0.5, 2.0),
        "lengths": draw_lengths(jax.random.fold_in(keys[5], 71), 0),
        "slot_order": draw_slot_order(jax.random.fold_in(keys[5], 71), 0),
    }


def cholesky_solve(matrix, target):
    factor = jnp.linalg.cholesky(matrix)
    halfway = lax.linalg.triangular_solve(factor, target, left_side=True, lower=True)
    return lax.linalg.triangular_solve(factor, halfway, left_side=True, lower=True, transpose_a=True)

def inner(first, second):
    return jnp.einsum('kri,kti->rt', first, second, precision=lax.Precision.HIGHEST)

def combine(field, matrix):
    return jnp.einsum('kri,rt->kti', field, matrix, precision=lax.Precision.HIGHEST)

def reference(operators, forces, weights, lengths, slot_order):
    breadth = forces.shape[2]
    chain = jnp.arange(NSUB, dtype=jnp.int32)
    effective = jnp.where(chain < NSUB - 1, lengths, 0)
    positions = jnp.arange(breadth, dtype=jnp.int32)
    live_mask = (positions[None, :] < effective[:, None]).astype(jnp.float32)[:, None, :]
    inverse = jnp.argsort(slot_order, axis=1).astype(jnp.int32)

    def operate(field):
        turned = jnp.take_along_axis(field, slot_order[:, None, :], axis=2)
        left_input = jnp.concatenate([jnp.zeros_like(turned[:1]), turned[:-1]], axis=0)
        inputs = jnp.concatenate([left_input, field], axis=2).astype(jnp.bfloat16)

        def single(pair):
            return jnp.dot(pair[0].astype(jnp.float32), pair[1].astype(jnp.float32), preferred_element_type=jnp.float32)
        products = lax.map(single, (inputs, operators))
        left_part = products[:, :, :breadth]
        right_part = products[:, :, breadth:]
        returned = jnp.concatenate([left_part[1:], jnp.zeros_like(left_part[:1])], axis=0)
        return live_mask * (right_part + jnp.take_along_axis(returned, inverse[:, None, :], axis=2))
    residual = live_mask * forces
    solution = jnp.zeros_like(residual)
    search = weights[:, None, :] * residual
    for iteration in range(ITERS):
        image = operate(search)
        curvature = inner(search, image)
        projection = inner(search, residual)
        alpha = cholesky_solve(curvature, projection)
        solution = solution + combine(search, alpha)
        residual = residual - combine(image, alpha)
        if iteration + 1 < ITERS:
            scaled = weights[:, None, :] * residual
            cross = inner(image, scaled)
            beta = -cholesky_solve(curvature, cross)
            search = scaled + combine(search, beta)
    return (solution, residual)
```

```python
import jax
import jax.numpy as jnp
from jax import lax
from jax.experimental import pallas as pl
from jax.experimental.pallas import tpu as pltpu
from jax.sharding import Mesh
from jax.sharding import PartitionSpec as P

GRP_DEV = ("grp_0", "grp_1", "grp_2", "dev")
F32 = jnp.float32
BF16 = jnp.bfloat16
HI = lax.Precision.HIGHEST
R = 32
B = 512
VM = pl.BlockSpec(memory_space=pltpu.VMEM)


def call(body, outs, n_in, smem=(), flops=10**8):
    return pl.pallas_call(
        body,
        out_shape=[jax.ShapeDtypeStruct(s, d) for s, d in outs],
        in_specs=[
            pl.BlockSpec(memory_space=pltpu.SMEM) if i in smem else VM for i in range(n_in)
        ],
        out_specs=[VM] * len(outs),
        compiler_params=pltpu.CompilerParams(vmem_limit_bytes=16 * 2**20),
        cost_estimate=pl.CostEstimate(flops=flops, bytes_accessed=2**20, transcendentals=0),
    )


def split(x):
    high = x.astype(BF16)
    return high, (x - high.astype(F32)).astype(BF16)


def pick(x, index):
    rows = x.shape[0]
    parts = []
    for out in range(B // 128):
        spread = jnp.broadcast_to(index[:, out * 128 : (out + 1) * 128], (rows, 128))
        low, high = spread & 127, spread >> 7
        part = None
        for source in range(B // 128):
            got = jnp.take_along_axis(
                x[:, source * 128 : (source + 1) * 128],
                low,
                axis=1,
                mode="promise_in_bounds",
            )
            part = got if part is None else jnp.where(high == source, got, part)
        parts.append(part)
    return jnp.concatenate(parts, axis=1)


def inverse_row(index):
    lane = lax.broadcasted_iota(jnp.int32, (128, 128), 1).astype(F32)
    place = lax.broadcasted_iota(jnp.int32, (128, 128), 0).astype(F32)
    values = index.astype(F32)
    sums = [None] * (B // 128)
    for source in range(B // 128):
        chunk = jnp.broadcast_to(values[:, source * 128 : (source + 1) * 128], (128, 128))
        column = chunk.T
        for out in range(B // 128):
            hit = jnp.where(column == lane + 128.0 * out, place + 128.0 * source, 0.0)
            sums[out] = hit if sums[out] is None else sums[out] + hit
    return jnp.concatenate([jnp.sum(s, axis=0, keepdims=True) for s in sums], axis=1)


def mm(x, y):
    return jnp.dot(x, y, preferred_element_type=F32)


def gram(x, y):
    return lax.dot_general(
        x, y, (((1,), (1,)), ((), ())), precision=HI, preferred_element_type=F32
    )


def begin(lens, forces, weights, order, r0, s0, rows, send):
    place = 0
    for axis in GRP_DEV:
        place = place * lax.axis_size(axis) + lax.axis_index(axis)
    lane = lax.broadcasted_iota(jnp.int32, (1, B), 1)
    for i in range(2):
        k = place * 2 + i
        live = jnp.where(k < lens.shape[0] - 1, lens[k], 0)
        mask = (lane < live).astype(F32)
        rows[i : i + 1, :] = mask
        rows[2 + i : 3 + i, :] = mask * weights[i : i + 1, :]
        field = mask * forces[i]
        r0[i] = field
        s0[i] = weights[i : i + 1, :] * field
    rows[4:8, :] = jnp.zeros((4, B), F32)
    stacked = jnp.concatenate([s0[1], jnp.broadcast_to(rows[3:4, :], (16, B))], axis=0)
    turned = pick(stacked, order[1:2, :])
    high, low = split(turned[:R])
    send[0:R, :] = high
    send[R : 2 * R, :] = low
    w = turned[R:]
    w1 = w.astype(BF16).astype(F32)
    w2 = (w - w1).astype(BF16).astype(F32)
    w3 = w - w1 - w2
    row = lax.broadcasted_iota(jnp.int32, (16, B), 0)
    send[2 * R : 2 * R + 16, :] = jnp.where(
        row == 0, w1, jnp.where(row == 1, w2, jnp.where(row == 2, w3, 0.0))
    ).astype(BF16)


def local_products(ops, s0, order, prod_b, part_a, forward, inv):
    inv[...] = jnp.concatenate(
        [inverse_row(order[0:1, :]), inverse_row(order[1:2, :]), jnp.zeros((6, B), F32)], axis=0
    ).astype(jnp.int32)
    t1, t2 = split(pick(s0[0], order[0:1, :]))
    b1, b2 = split(s0[1])
    x = jnp.concatenate(
        [jnp.concatenate([t1, b1], axis=1), jnp.concatenate([t2, b2], axis=1)], axis=0
    )
    prod = mm(x, ops[1])
    prod_b[...] = prod
    forward[...] = pick(prod[:R, B:], order[1:2, :])
    a1, a2 = split(s0[0])
    part_a[...] = mm(jnp.concatenate([a1, a2], axis=0), ops[0, B:, :])


def left_of_a(ops, came, part_a, back, left_low):
    left = part_a[:, :B] + mm(came[0 : 2 * R, :], ops[0, :B, :B])
    back[...] = left[:R]
    left_low[...] = left[R:]


def second_local(
    ops, came, came_right, part_a, back, left_low, prod_b, inv, rows, order, r0, s0,
    q_a, d_a, u_a, v_a, t_ua, part2_b, send_back, gpart,
):
    right = part_a[:, B:] + mm(came[0 : 2 * R, :], ops[0, :B, B:])
    both = right + pick(prod_b[:, :B], inv[0:1, :])
    q = rows[0:1, :] * both[:R]
    q_a[...] = q
    d_a[...] = rows[0:1, :] * both[R:]
    u = rows[2:3, :] * q
    u_a[...] = u
    w = came[2 * R : 2 * R + 16, :].astype(F32)
    w_prev = w[0:1] + w[1:2] + w[2:3]
    u_prev = w_prev * (came_right[...] + back[...])
    p1, p2 = split(u_prev)
    a1, a2 = split(u)
    x = jnp.concatenate(
        [jnp.concatenate([p1, a1], axis=1), jnp.concatenate([p2, a2], axis=1)], axis=0
    )
    prod = mm(x, ops[0])
    prod = prod[:R] + prod[R:]
    send_back[0:R, :] = prod[:, :B]
    send_back[R:, :] = left_low[...]
    v_a[...] = prod[:, B:]
    turned = pick(u, order[0:1, :])
    t_ua[...] = turned
    t1, t2 = split(turned)
    part = mm(jnp.concatenate([t1, t2], axis=0), ops[1, :B, :])
    part2_b[...] = part[:R] + part[R:]
    g4 = gram(jnp.concatenate([u_prev, u], axis=1), prod)
    g13 = gram(jnp.concatenate([s0[0], u], axis=0), q)
    g2 = gram(s0[0], r0[0]) + gram(s0[1], r0[1])
    gpart[...] = jnp.concatenate([g13[:R], g2, g13[R:], g4], axis=1)


def grams(ops, came_back, prod_b, inv, rows, s0, t_ua, part2_b, gpart, q_b, u_b, prod2_b, out):
    q = rows[1:2, :] * (prod_b[0:R, B:] + pick(came_back[...], inv[1:2, :]))
    q_b[...] = q
    u = rows[3:4, :] * q
    u_b[...] = u
    b1, b2 = split(u)
    prod = mm(jnp.concatenate([b1, b2], axis=0), ops[1, B:, :])
    prod = part2_b[...] + prod[:R] + prod[R:]
    prod2_b[...] = prod
    g4 = gram(jnp.concatenate([t_ua[...], u], axis=1), prod)
    g13 = gram(jnp.concatenate([s0[1], u], axis=0), q)
    out[...] = gpart[...] + jnp.concatenate(
        [g13[:R], jnp.zeros((R, R), F32), g13[R:], g4], axis=1
    )


def eliminate(m):
    row = lax.broadcasted_iota(jnp.int32, (R, 1), 0)
    for j in range(R):
        line = m[j : j + 1, :] / m[j : j + 1, j : j + 1]
        m = jnp.where(row == j, line, m - m[:, j : j + 1] * line)
    return m


def hdot(x, y):
    return jnp.dot(x, y, precision=HI, preferred_element_type=F32)


def finish(
    parts, came, prod_b, prod2_b, inv, rows, r0, s0, q_a, q_b, d_a, u_a, u_b, v_a, x_out, r_out
):
    g = parts[0]
    for i in range(1, parts.shape[0]):
        g = g + parts[i]
    gt = g.T
    g1, g2, g3, g4 = (g[:, i * R : (i + 1) * R] for i in range(4))
    g1t = gt[0:R, :]
    g4t = gt[3 * R : 4 * R, :]
    m = eliminate(jnp.concatenate([0.5 * (g1 + g1t), g2, g1t, g3], axis=1))
    alpha = m[:, R : 2 * R]
    eye = (
        lax.broadcasted_iota(jnp.int32, (R, R), 0) == lax.broadcasted_iota(jnp.int32, (R, R), 1)
    ).astype(F32)
    grown = eye - m[:, 2 * R : 3 * R] + hdot(m[:, 3 * R :], alpha)
    cross = g1t - hdot(g3, alpha)
    top = hdot(g1, grown) - hdot(g3, alpha)
    bottom = hdot(g3, grown) - hdot(0.5 * (g4 + g4t), alpha)
    flip = jnp.concatenate([grown, alpha, jnp.zeros((R, 2 * R), F32)], axis=1).T
    grown_t, alpha_t = flip[0:R, :], flip[R : 2 * R, :]
    curve = hdot(grown_t, top) - hdot(alpha_t, bottom)
    target = hdot(grown_t, g2 - hdot(g1, alpha)) - hdot(alpha_t, cross)
    curve_t = jnp.concatenate([curve, jnp.zeros((R, 3 * R), F32)], axis=1).T[0:R, :]
    m = eliminate(
        jnp.concatenate([0.5 * (curve + curve_t), target, jnp.zeros((R, 2 * R), F32)], axis=1)
    )
    alpha1 = m[:, R : 2 * R]
    onto_d = hdot(grown, alpha1)
    onto_u = hdot(alpha, alpha1)
    onto_s = alpha + onto_d
    coefficients = jnp.concatenate([onto_s, onto_d, onto_u, jnp.zeros((R, R), F32)], axis=1).T
    cs, cd, cu = coefficients[0:R], coefficients[R : 2 * R], coefficients[2 * R : 3 * R]
    d_right = rows[1:2, :] * (prod_b[R:, B:] + pick(came[R:, :], inv[1:2, :]))
    v_right = rows[1:2, :] * (prod2_b[:, B:] + pick(came[0:R, :], inv[1:2, :]))
    v_left = rows[0:1, :] * (v_a[...] + pick(prod2_b[:, :B], inv[0:1, :]))
    for i, q, d, u, v in ((0, q_a, d_a[...], u_a, v_left), (1, q_b, d_right, u_b, v_right)):
        x_out[i] = hdot(cs, s0[i]) - hdot(cu, u[...])
        r_out[i] = r0[i] - hdot(cs, q[...]) - hdot(cd, d) + hdot(cu, v)


def shifted(block, axes_size, distance):
    route = [(i, i + distance) for i in range(axes_size) if 0 <= i + distance < axes_size]
    return lax.ppermute(block, GRP_DEV, route)


def gathered(block, axes):
    spread = jnp.broadcast_to(block[None], (lax.axis_size(axes), *block.shape))
    return lax.all_to_all(spread, axes, 0, 0, tiled=True)


def body(operators, forces, weights, lengths, slot_order):
    devices = lax.axis_size(GRP_DEV)
    field, pair = ((R, B), F32), ((2, R, B), F32)
    r0, s0, rows, send = call(
        begin, [pair, pair, ((8, B), F32), ((2 * R + 16, B), BF16)], 4, smem=(0,)
    )(lengths, forces, weights, slot_order)
    came = shifted(send, devices, 1)
    prod_b, part_a, forward, inv = call(
        local_products,
        [((2 * R, 2 * B), F32), ((2 * R, 2 * B), F32), field, ((8, B), jnp.int32)],
        3,
    )(operators, s0, slot_order)
    came_right = shifted(forward, devices, 1)
    back, left_low = call(left_of_a, [field, field], 3)(operators, came, part_a)
    came_back = shifted(back, devices, -1)
    q_a, d_a, u_a, v_a, t_ua, part2_b, send_back, gpart = call(
        second_local,
        [field] * 5 + [((R, 2 * B), F32), ((2 * R, B), F32), ((R, 4 * R), F32)],
        12,
    )(
        operators, came, came_right, part_a, back, left_low, prod_b, inv, rows, slot_order, r0, s0
    )
    came_last = shifted(send_back, devices, -1)
    q_b, u_b, prod2_b, local = call(
        grams, [field, field, ((R, 2 * B), F32), ((R, 4 * R), F32)], 9
    )(operators, came_back, prod_b, inv, rows, s0, t_ua, part2_b, gpart)
    total = jnp.sum(gathered(local, ("grp_2", "dev")), axis=0)
    total = jnp.sum(gathered(total, "grp_0"), axis=0)
    parts = gathered(total, "grp_1")
    solution, residual = call(finish, [pair, pair], 14)(
        parts, came_last, prod_b, prod2_b, inv, rows, r0, s0, q_a, q_b, d_a, u_a, u_b, v_a
    )
    return (solution, residual)


def solution(mesh):
    split_mesh = Mesh(
        mesh.devices.reshape(8, 12, 2, mesh.shape["dev"]), ("grp_0", "grp_1", "grp_2", "dev")
    )
    return jax.shard_map(
        body,
        mesh=split_mesh,
        in_specs=(
            P(GRP_DEV, None, None),
            P(GRP_DEV, None, None),
            P(GRP_DEV, None),
            P(),
            P(GRP_DEV, None),
        ),
        out_specs=(P(GRP_DEV, None, None), P(GRP_DEV, None, None)),
        check_vma=False,
    )
```
